32 devices in a mesh: row: 4 (over y, core), col: 8 (over z, x).
Axes of the slice: x: 2, y: 2, z: 4, core: 2. Of those that a mesh axis runs over, the one named last changes fastest.
Arguments:
- gradient: bfloat16 [3584, 12288], P('row', 'col'), may hold values from -54 to 54
- momentum: float32 [3584, 12288], P('row', 'col'), may hold values from -54 to 54
Outputs:
- update_matrix: bfloat16 [3584, 12288], P('row', 'col')
- new_momentum: float32 [3584, 12288], P('row', 'col')
The draws below stay inside these ranges and needn't reach their ends.
All inputs are finite; a program needn't handle non-finite values.
Results may differ from the reference program's by a relative error of at most 0.013.
Values may be sent and summed in bfloat16 or wider, within the bound.
A program may use at most 128 MiB of HBM per device.

```python
import math
import jax
import jax.numpy as jnp

M = 3584
N = 12288
ITERS = 2


def ramped_rows(key):
    first, second = jax.random.split(key)
    position = jnp.arange(M).astype(jnp.float32) / M
    trend = jnp.exp(position * math.log(3.0))[:, None]
    factor = jnp.exp(jax.random.uniform(first, (M, 1), jnp.float32) * math.log(3.0))
    noise = jnp.clip(jax.random.normal(second, (M, N), jnp.float32), -4.0, 4.0)
    values = noise + 0.5 * jnp.roll(noise, M // 2, axis=0)
    return values * trend * factor


def draw_gradient(key, part):
    return ramped_rows(jax.random.fold_in(key, 11)).astype(jnp.bfloat16)


def draw_momentum(key, part):
    return ramped_rows(jax.random.fold_in(key, 23)).astype(jnp.float32)


def setup_inputs(seed: int = 0) -> dict:
    key_of = jax.random.split(jax.random.key(seed), 3)
    gradient = draw_gradient(jax.random.fold_in(key_of[2], 71), 0)
    momentum = draw_momentum(jax.random.fold_in(key_of[2], 71), 0)
    return {"gradient": gradient, "momentum": momentum}


MOMENTUM_DECAY = 0.95
EPSILON = 1e-07
COEF_LINEAR = 3.4445
COEF_CUBIC = -4.775
COEF_QUINTIC = 2.0315

def reference(gradient, momentum):
    grad32 = gradient.astype(jnp.float32)
    buffer = MOMENTUM_DECAY * momentum + grad32
    nesterov = grad32 + MOMENTUM_DECAY * buffer
    base = nesterov.astype(jnp.bfloat16)
    raw = jnp.dot(base, base.T, preferred_element_type=jnp.float32)
    quartic = jnp.sum(raw * raw)
    scale = 1.0 / jnp.sqrt(jnp.sqrt(quartic) + EPSILON)
    iterate = (base.astype(jnp.float32) * scale).astype(jnp.bfloat16)
    combined = iterate.astype(jnp.float32)
    for iteration in range(ITERS):
        if iteration == 0:
            gram = (raw * (scale * scale)).astype(jnp.bfloat16)
        else:
            gram = jnp.dot(iterate, iterate.T, preferred_element_type=jnp.float32).astype(jnp.bfloat16)
        product = jnp.dot(gram, iterate, preferred_element_type=jnp.float32)
        second = jnp.dot(gram, product.astype(jnp.bfloat16), preferred_element_type=jnp.float32)
        combined = COEF_LINEAR * iterate.astype(jnp.float32) + COEF_CUBIC * product + COEF_QUINTIC * second
        if iteration + 1 < ITERS:
            iterate = combined.astype(jnp.bfloat16)
    update_matrix = (combined * (0.2 * math.sqrt(max(M, N)))).astype(jnp.bfloat16)
    return (update_matrix, buffer)
```

```python
import functools
import math

import jax
import jax.numpy as jnp
from jax import lax
from jax.experimental import pallas as pl
from jax.experimental.pallas import tpu as pltpu
from jax.sharding import PartitionSpec as P

ITERS = 2

MOMENTUM_DECAY = 0.95
EPSILON = 1e-07
COEF_LINEAR = 3.4445
COEF_CUBIC = -4.775
COEF_QUINTIC = 2.0315


def outer_rows(left, right):
    return lax.dot_general(
        left, right, (((1,), (1,)), ((), ())), preferred_element_type=jnp.float32
    )


def chain_kernel(tile, factor, scale_ref, gram_ref, x_ref, out_ref, first, one, two, rough, exact, total):
    scale = scale_ref[0, 0]
    square = scale * scale
    size = gram_ref.shape[0]

    def times_gram(source, finish):
        @pl.loop(0, size // tile)
        def _(step):
            columns = pl.ds(pl.multiple_of(step * tile, tile), tile)
            value = jnp.dot(
                source[...], gram_ref[:, columns], preferred_element_type=jnp.float32
            )
            finish(columns, value * square)

    def polynomial(source, target):
        def keep(columns, value):
            exact[:, columns] = value
            rough[:, columns] = value.astype(jnp.bfloat16)

        def combine(columns, value):
            target[:, columns] = (
                COEF_LINEAR * source[:, columns].astype(jnp.float32)
                + COEF_CUBIC * exact[:, columns]
                + COEF_QUINTIC * value
            ).astype(jnp.bfloat16)

        times_gram(source, keep)
        times_gram(rough, combine)

    polynomial(x_ref, first)
    polynomial(first, one)
    polynomial(one, two)

    def after_product(columns, value):
        total[:, columns] = (
            COEF_LINEAR * first[:, columns].astype(jnp.float32) + COEF_CUBIC * value
        )
        one[:, columns] = value.astype(jnp.bfloat16)

    times_gram(two, after_product)
    polynomial(one, two)
    polynomial(two, one)

    def after_second(columns, value):
        out_ref[:, columns] = (
            (total[:, columns] + COEF_QUINTIC * value) * (scale * factor)
        ).astype(jnp.bfloat16)

    times_gram(one, after_second)


def chain(scale, gram, slab, factor):
    width, size = slab.shape
    tile = 512 if size % 512 == 0 else size
    vmem = pl.BlockSpec(memory_space=pltpu.VMEM)
    half = pltpu.VMEM((width, size), jnp.bfloat16)
    full = pltpu.VMEM((width, size), jnp.float32)
    return pl.pallas_call(
        functools.partial(chain_kernel, tile, factor),
        out_shape=jax.ShapeDtypeStruct((width, size), jnp.bfloat16),
        in_specs=[pl.BlockSpec(memory_space=pltpu.SMEM), vmem, vmem],
        out_specs=vmem,
        scratch_shapes=[half, half, half, half, full, full],
        compiler_params=pltpu.CompilerParams(vmem_limit_bytes=62 * 1024 * 1024),
        name="chain",
    )(scale.reshape(1, 1), gram, slab)


def assembled(shares, rows, block):
    half = block // 2
    middle = rows // 2

    def at(i, j):
        offset = (i - j) % rows
        if offset < middle:
            return shares[j, offset * block : (offset + 1) * block]
        if offset > middle:
            return at(j, i).T
        low, high = min(i, j), max(i, j)
        value = jnp.concatenate([shares[low, -half:], shares[high, -half:]], axis=0)
        return value if i == low else value.T

    return jnp.concatenate(
        [
            jnp.concatenate([at(i, j) for j in range(rows)], axis=1)
            for i in range(rows)
        ],
        axis=0,
    )


def per_device(factor, gradient, momentum):
    rows = lax.axis_size("row")
    grad32 = gradient.astype(jnp.float32)
    buffer = MOMENTUM_DECAY * momentum + grad32
    nesterov = grad32 + MOMENTUM_DECAY * buffer
    base = nesterov.astype(jnp.bfloat16)
    block = base.shape[0]
    half = block // 2
    middle = rows // 2
    me = lax.axis_index("row")
    panel = lax.all_gather(base, "row", axis=0, tiled=True)

    def rows_of(offset):
        start = ((me + offset) % rows) * block
        return lax.dynamic_slice_in_dim(panel, start, block, axis=0)

    parts = [outer_rows(base, base)]
    for offset in range(1, middle):
        parts.append(outer_rows(rows_of(offset), base))
    facing = rows_of(middle)
    lower = me < middle
    parts.append(
        outer_rows(
            jnp.where(lower, base[:half], facing[half:]), jnp.where(lower, facing, base)
        )
    )
    partial_value = jnp.concatenate([part.astype(jnp.bfloat16) for part in parts], axis=0)
    share = lax.psum_scatter(partial_value, "col", scatter_dimension=0, tiled=True)
    shares = lax.all_gather(share, ("row", "col"), axis=0, tiled=True)
    shares = shares.reshape(rows, -1, block)
    gram = assembled(shares, rows, block)
    quartic = jnp.sum(jnp.square(gram.astype(jnp.float32)))
    scale = 1.0 / jnp.sqrt(jnp.sqrt(quartic) + EPSILON)

    width = panel.shape[1] // rows
    slab = lax.dynamic_slice_in_dim(panel, me * width, width, axis=1).T
    update = chain(scale, gram, slab, factor).T
    update = lax.all_to_all(update, "row", 0, 1, tiled=True)
    return (update, buffer)


def solution(mesh):
    def whole(gradient, momentum):
        factor = 0.2 * math.sqrt(max(gradient.shape))
        return jax.shard_map(
            functools.partial(per_device, factor),
            mesh=mesh,
            in_specs=(P("row", "col"), P("row", "col")),
            out_specs=(P("row", "col"), P("row", "col")),
            check_vma=False,
        )(gradient, momentum)

    return whole
```

```python
import functools
import math

import jax
import jax.numpy as jnp
from jax import lax
from jax.experimental import pallas as pl
from jax.experimental.pallas import tpu as pltpu
from jax.sharding import PartitionSpec as P

ITERS = 2

MOMENTUM_DECAY = 0.95
EPSILON = 1e-07
COEF_LINEAR = 3.4445
COEF_CUBIC = -4.775
COEF_QUINTIC = 2.0315


def outer_rows(left, right):
    return lax.dot_general(
        left, right, (((1,), (1,)), ((), ())), preferred_element_type=jnp.float32
    )


def direct_blocks(rows, block):
    if rows == 1:
        return [(0, 0, block, 0, 0)]
    half = block // 2
    middle = rows // 2
    found = []
    for j in range(rows):
        for offset in range(middle):
            i = (j + offset) % rows
            found.append((j, offset * block, block, i * block, j * block))
        low, high = min(j, (j + middle) % rows), max(j, (j + middle) % rows)
        top = low * block + (0 if j == low else half)
        found.append((j, middle * block, half, top, high * block))
    return found


def mirrored_blocks(rows):
    if rows == 1:
        return []
    middle = rows // 2
    pairs = [((j + k) % rows, j) for j in range(rows) for k in range(1, middle)]
    return pairs + [(low, low + middle) for low in range(middle)]


def chain_kernel(
    tile, factor, rows, shares_ref, x_ref, out_ref, gram_ref, first, one, two, rough, exact, total, sems
):
    size = gram_ref.shape[0]
    block = size // rows
    stride = shares_ref.shape[0] // rows
    strip = 128
    copies = []
    for number, (owner, start, height, row, column) in enumerate(direct_blocks(rows, block)):
        copies.append(
            pltpu.make_async_copy(
                shares_ref.at[pl.ds(owner * stride + start, height), :],
                gram_ref.at[pl.ds(row, height), pl.ds(column, block)],
                sems.at[number],
            )
        )
    for copy in copies:
        copy.start()
    for copy in copies:
        copy.wait()

    def squares(i, j, mirror):
        def body(step, carry):
            lanes = pl.ds(pl.multiple_of(j * block + step * strip, strip), strip)
            piece = gram_ref[pl.ds(i * block, block), lanes]
            if mirror:
                gram_ref[lanes, pl.ds(i * block, block)] = piece.T
            wide = piece.astype(jnp.float32)
            return carry + jnp.sum(wide * wide, axis=0, keepdims=True)

        return lax.fori_loop(0, block // strip, body, jnp.zeros((1, strip), jnp.float32))

    diagonal = sum(squares(i, i, False) for i in range(rows))
    others = sum(squares(i, j, True) for i, j in mirrored_blocks(rows)) + jnp.zeros_like(diagonal)
    quartic = jnp.sum(diagonal + 2.0 * others, axis=1, keepdims=True)
    scale = 1.0 / jnp.sqrt(jnp.sqrt(quartic) + EPSILON)
    square = scale * scale

    def times_gram(source, finish):
        @pl.loop(0, size // tile)
        def _(step):
            columns = pl.ds(pl.multiple_of(step * tile, tile), tile)
            value = jnp.dot(
                source[...], gram_ref[:, columns], preferred_element_type=jnp.float32
            )
            finish(columns, value * square)

    def polynomial(source, target):
        def keep(columns, value):
            exact[:, columns] = value
            rough[:, columns] = value.astype(jnp.bfloat16)

        def combine(columns, value):
            target[:, columns] = (
                COEF_LINEAR * source[:, columns].astype(jnp.float32)
                + COEF_CUBIC * exact[:, columns]
                + COEF_QUINTIC * value
            ).astype(jnp.bfloat16)

        times_gram(source, keep)
        times_gram(rough, combine)

    width = x_ref.shape[1]
    lanes_step = 128 if width % 128 == 0 else width

    @pl.loop(0, size // strip)
    def _(step):
        chunk = pl.ds(pl.multiple_of(step * strip, strip), strip)
        for lane in range(0, width, lanes_step):
            two[lane : lane + lanes_step, chunk] = x_ref[chunk, lane : lane + lanes_step].T

    polynomial(two, first)
    polynomial(first, one)
    polynomial(one, two)

    def after_product(columns, value):
        total[:, columns] = (
            COEF_LINEAR * first[:, columns].astype(jnp.float32) + COEF_CUBIC * value
        )
        one[:, columns] = value.astype(jnp.bfloat16)

    times_gram(two, after_product)
    polynomial(one, two)
    polynomial(two, one)

    def after_second(columns, value):
        two[:, columns] = (
            (total[:, columns] + COEF_QUINTIC * value) * (scale * factor)
        ).astype(jnp.bfloat16)

    times_gram(one, after_second)

    @pl.loop(0, size // strip)
    def _(step):
        chunk = pl.ds(pl.multiple_of(step * strip, strip), strip)
        for lane in range(0, width, lanes_step):
            out_ref[chunk, lane : lane + lanes_step] = two[lane : lane + lanes_step, chunk].T


def chain(shares, slab, factor, rows):
    size, width = slab.shape
    tile = 512 if size % 512 == 0 else size
    vmem = pl.BlockSpec(memory_space=pltpu.VMEM)
    half = pltpu.VMEM((width, size), jnp.bfloat16)
    full = pltpu.VMEM((width, size), jnp.float32)
    count = rows * (rows // 2 + 1)
    return pl.pallas_call(
        functools.partial(chain_kernel, tile, factor, rows),
        out_shape=jax.ShapeDtypeStruct((size, width), jnp.bfloat16),
        in_specs=[pl.BlockSpec(memory_space=pl.ANY), vmem],
        out_specs=vmem,
        scratch_shapes=[pltpu.VMEM((size, size), jnp.bfloat16)]
        + [half, half, half, half, full, full, pltpu.SemaphoreType.DMA((count,))],
        compiler_params=pltpu.CompilerParams(vmem_limit_bytes=63 * 1024 * 1024),
        name="chain",
    )(shares, slab)


def assembled(shares, rows, block):
    half = block // 2
    middle = rows // 2

    def at(i, j):
        offset = (i - j) % rows
        if offset < middle:
            return shares[j, offset * block : (offset + 1) * block]
        if offset > middle:
            return at(j, i).T
        low, high = min(i, j), max(i, j)
        value = jnp.concatenate([shares[low, -half:], shares[high, -half:]], axis=0)
        return value if i == low else value.T

    return jnp.concatenate(
        [
            jnp.concatenate([at(i, j) for j in range(rows)], axis=1)
            for i in range(rows)
        ],
        axis=0,
    )


def per_device(factor, gradient, momentum):
    rows = lax.axis_size("row")
    grad32 = gradient.astype(jnp.float32)
    buffer = MOMENTUM_DECAY * momentum + grad32
    nesterov = grad32 + MOMENTUM_DECAY * buffer
    base = nesterov.astype(jnp.bfloat16)
    block = base.shape[0]
    half = block // 2
    middle = rows // 2
    me = lax.axis_index("row")
    panel = lax.all_gather(base, "row", axis=0, tiled=True)

    def rows_of(offset):
        start = ((me + offset) % rows) * block
        return lax.dynamic_slice_in_dim(panel, start, block, axis=0)

    parts = [outer_rows(base, base)]
    for offset in range(1, middle):
        parts.append(outer_rows(rows_of(offset), base))
    facing = rows_of(middle)
    lower = me < middle
    parts.append(
        outer_rows(
            jnp.where(lower, base[:half], facing[half:]), jnp.where(lower, facing, base)
        )
    )
    partial_value = jnp.concatenate([part.astype(jnp.bfloat16) for part in parts], axis=0)
    share = lax.psum_scatter(partial_value, "col", scatter_dimension=0, tiled=True)
    shares = lax.all_gather(share, ("row", "col"), axis=0, tiled=True)
    parts = rows
    if block % 128:
        shares = assembled(shares.reshape(rows, -1, block), rows, block)
        parts = 1

    width = panel.shape[1] // rows
    slab = lax.dynamic_slice_in_dim(panel, me * width, width, axis=1)
    update = chain(shares, slab, factor, parts)
    update = lax.all_to_all(update, "row", 0, 1, tiled=True)
    return (update, buffer)


def solution(mesh):
    def whole(gradient, momentum):
        factor = 0.2 * math.sqrt(max(gradient.shape))
        return jax.shard_map(
            functools.partial(per_device, factor),
            mesh=mesh,
            in_specs=(P("row", "col"), P("row", "col")),
            out_specs=(P("row", "col"), P("row", "col")),
            check_vma=False,
        )(gradient, momentum)

    return whole
```

```python
import functools
import math

import jax
import jax.numpy as jnp
from jax import lax
from jax.experimental import pallas as pl
from jax.experimental.pallas import tpu as pltpu
from jax.sharding import PartitionSpec as P

ITERS = 2

MOMENTUM_DECAY = 0.95
EPSILON = 1e-07
COEF_LINEAR = 3.4445
COEF_CUBIC = -4.775
COEF_QUINTIC = 2.0315


def outer_rows(left, right):
    return lax.dot_general(
        left, right, (((1,), (1,)), ((), ())), preferred_element_type=jnp.float32
    )


def direct_blocks(rows, block):
    if rows == 1:
        return [(0, 0, block, 0, 0)]
    half = block // 2
    middle = rows // 2
    found = []
    for j in range(rows):
        for offset in range(middle):
            i = (j + offset) % rows
            found.append((j, offset * block, block, i * block, j * block))
        low, high = min(j, (j + middle) % rows), max(j, (j + middle) % rows)
        top = low * block + (0 if j == low else half)
        found.append((j, middle * block, half, top, high * block))
    return found


def mirrored_blocks(rows):
    if rows == 1:
        return []
    middle = rows // 2
    pairs = [((j + k) % rows, j) for j in range(rows) for k in range(1, middle)]
    return pairs + [(low, low + middle) for low in range(middle)]


def chain_kernel(
    tile, factor, rows, shares_ref, x_ref, out_ref, gram_ref, first, one, two, rough, exact, total, sems
):
    size = gram_ref.shape[0]
    block = size // rows
    stride = shares_ref.shape[0] // rows
    strip = 128
    copies = []
    for number, (owner, start, height, row, column) in enumerate(direct_blocks(rows, block)):
        copies.append(
            pltpu.make_async_copy(
                shares_ref.at[pl.ds(owner * stride + start, height), :],
                gram_ref.at[pl.ds(row, height), pl.ds(column, block)],
                sems.at[number],
            )
        )
    for copy in copies:
        copy.start()
    for copy in copies:
        copy.wait()

    def squares(i, j, mirror):
        def body(step, carry):
            lanes = pl.ds(pl.multiple_of(j * block + step * strip, strip), strip)
            piece = gram_ref[pl.ds(i * block, block), lanes]
            if mirror:
                gram_ref[lanes, pl.ds(i * block, block)] = piece.T
            wide = piece.astype(jnp.float32)
            return carry + jnp.sum(wide * wide, axis=0, keepdims=True)

        return lax.fori_loop(0, block // strip, body, jnp.zeros((1, strip), jnp.float32))

    diagonal = sum(squares(i, i, False) for i in range(rows))
    others = sum(squares(i, j, True) for i, j in mirrored_blocks(rows)) + jnp.zeros_like(diagonal)
    quartic = jnp.sum(diagonal + 2.0 * others, axis=1, keepdims=True)
    scale = 1.0 / jnp.sqrt(jnp.sqrt(quartic) + EPSILON)
    square = scale * scale

    def times_gram(source, finish):
        @pl.loop(0, size // tile)
        def _(step):
            columns = pl.ds(pl.multiple_of(step * tile, tile), tile)
            value = jnp.dot(
                source[...], gram_ref[:, columns], preferred_element_type=jnp.float32
            )
            finish(columns, value * square)

    def polynomial(source, target):
        def keep(columns, value):
            exact[:, columns] = value
            rough[:, columns] = value.astype(jnp.bfloat16)

        def combine(columns, value):
            target[:, columns] = (
                COEF_LINEAR * source[:, columns].astype(jnp.float32)
                + COEF_CUBIC * exact[:, columns]
                + COEF_QUINTIC * value
            ).astype(jnp.bfloat16)

        times_gram(source, keep)
        times_gram(rough, combine)

    width = x_ref.shape[1]
    lanes_step = 128 if width % 128 == 0 else width

    @pl.loop(0, size // strip)
    def _(step):
        chunk = pl.ds(pl.multiple_of(step * strip, strip), strip)
        for lane in range(0, width, lanes_step):
            two[lane : lane + lanes_step, chunk] = x_ref[chunk, lane : lane + lanes_step].T

    polynomial(two, first)
    polynomial(first, one)
    polynomial(one, two)

    def after_product(columns, value):
        total[:, columns] = (
            COEF_LINEAR * first[:, columns].astype(jnp.float32) + COEF_CUBIC * value
        )
        one[:, columns] = value.astype(jnp.bfloat16)

    times_gram(two, after_product)
    polynomial(one, two)
    polynomial(two, one)

    def after_second(columns, value):
        two[:, columns] = (
            (total[:, columns] + COEF_QUINTIC * value) * (scale * factor)
        ).astype(jnp.bfloat16)

    times_gram(one, after_second)

    @pl.loop(0, size // strip)
    def _(step):
        chunk = pl.ds(pl.multiple_of(step * strip, strip), strip)
        for lane in range(0, width, lanes_step):
            out_ref[chunk, lane : lane + lanes_step] = two[lane : lane + lanes_step, chunk].T


def chain(shares, slab, factor, rows):
    size, width = slab.shape
    tile = 512 if size % 512 == 0 else size
    vmem = pl.BlockSpec(memory_space=pltpu.VMEM)
    half = pltpu.VMEM((width, size), jnp.bfloat16)
    full = pltpu.VMEM((width, size), jnp.float32)
    count = rows * (rows // 2 + 1)
    return pl.pallas_call(
        functools.partial(chain_kernel, tile, factor, rows),
        out_shape=jax.ShapeDtypeStruct((size, width), jnp.bfloat16),
        in_specs=[pl.BlockSpec(memory_space=pl.ANY), vmem],
        out_specs=vmem,
        scratch_shapes=[pltpu.VMEM((size, size), jnp.bfloat16)]
        + [half, half, half, half, full, full, pltpu.SemaphoreType.DMA((count,))],
        compiler_params=pltpu.CompilerParams(vmem_limit_bytes=63 * 1024 * 1024),
        name="chain",
    )(shares, slab)


def assembled(shares, rows, block):
    half = block // 2
    middle = rows // 2

    def at(i, j):
        offset = (i - j) % rows
        if offset < middle:
            return shares[j, offset * block : (offset + 1) * block]
        if offset > middle:
            return at(j, i).T
        low, high = min(i, j), max(i, j)
        value = jnp.concatenate([shares[low, -half:], shares[high, -half:]], axis=0)
        return value if i == low else value.T

    return jnp.concatenate(
        [
            jnp.concatenate([at(i, j) for j in range(rows)], axis=1)
            for i in range(rows)
        ],
        axis=0,
    )


def ring_kernel(partial_ref, out_ref, *scratch):
    landed, running, send_sems, recv_sems = scratch[:2], scratch[2:4], scratch[4], scratch[5]
    count = partial_ref.shape[0]
    column = lax.axis_index("col")
    odd, pair = lax.rem(column, 2), lax.div(column, 2)
    place = (1 - odd) * pair + odd * (count - 1 - pair)
    sign = 1 - 2 * lax.rem(lax.axis_index("row"), 2)
    ways = (sign, -sign)
    wide = landed[0].shape[2]
    lanes = (pl.ds(0, wide), pl.ds(wide, landed[1].shape[2]))

    def column_at(spot):
        spot = lax.rem(spot + 2 * count, count)
        back = lax.div(spot, count // 2)
        return (1 - back) * 2 * spot + back * (2 * (count - 1 - spot) + 1)

    barrier = pltpu.get_barrier_semaphore()
    for way in ways:
        pl.semaphore_signal(
            barrier,
            inc=1,
            device_id={"col": column_at(place + way)},
            device_id_type=pl.DeviceIdType.MESH,
        )
    pl.semaphore_wait(barrier, 2)

    def copy_of(step, k, source):
        return pltpu.make_async_remote_copy(
            src_ref=source,
            dst_ref=landed[k].at[step],
            send_sem=send_sems.at[k, step],
            recv_sem=recv_sems.at[k, step],
            device_id={"col": column_at(place + ways[k])},
            device_id_type=pl.DeviceIdType.MESH,
        )

    copies = []
    for k in range(2):
        source = partial_ref.at[column_at(place - ways[k]), :, lanes[k]]
        copies.append([copy_of(0, k, source)])
        copies[k][0].start()
    for step in range(count - 1):
        for k in range(2):
            copies[k][step].wait_recv()
            mine = partial_ref[column_at(place - ways[k] * (step + 2)), :, lanes[k]]
            value = landed[k][step].astype(jnp.float32) + mine.astype(jnp.float32)
            value = value.astype(jnp.bfloat16)
            if step < count - 2:
                running[k][step] = value
                copies[k].append(copy_of(step + 1, k, running[k].at[step]))
                copies[k][step + 1].start()
            else:
                out_ref[:, lanes[k]] = value
    for k in range(2):
        for copy in copies[k]:
            copy.wait_send()


def ring_sum(partial_value, count):
    block = partial_value.shape[1]
    height = partial_value.shape[0] // count
    wide = (block // 128 + 1) // 2 * 128
    vmem = pl.BlockSpec(memory_space=pltpu.VMEM)
    slots = [
        pltpu.VMEM((count - 1, height, width), jnp.bfloat16) for width in (wide, block - wide)
    ]
    sems = pltpu.SemaphoreType.DMA((2, count - 1))
    return pl.pallas_call(
        ring_kernel,
        out_shape=jax.ShapeDtypeStruct((height, block), jnp.bfloat16),
        in_specs=[vmem],
        out_specs=vmem,
        scratch_shapes=slots + slots + [sems, sems],
        compiler_params=pltpu.CompilerParams(
            collective_id=0, has_side_effects=True, vmem_limit_bytes=40 * 1024 * 1024
        ),
        name="ring_sum",
    )(partial_value.reshape(count, height, block))


def per_device(factor, gradient, momentum):
    rows = lax.axis_size("row")
    grad32 = gradient.astype(jnp.float32)
    buffer = MOMENTUM_DECAY * momentum + grad32
    nesterov = grad32 + MOMENTUM_DECAY * buffer
    base = nesterov.astype(jnp.bfloat16)
    block = base.shape[0]
    half = block // 2
    middle = rows // 2
    me = lax.axis_index("row")
    panel = lax.all_gather(base, "row", axis=0, tiled=True)

    def rows_of(offset):
        start = ((me + offset) % rows) * block
        return lax.dynamic_slice_in_dim(panel, start, block, axis=0)

    parts = [outer_rows(base, base)]
    for offset in range(1, middle):
        parts.append(outer_rows(rows_of(offset), base))
    facing = rows_of(middle)
    lower = me < middle
    parts.append(
        outer_rows(
            jnp.where(lower, base[:half], facing[half:]), jnp.where(lower, facing, base)
        )
    )
    partial_value = jnp.concatenate([part.astype(jnp.bfloat16) for part in parts], axis=0)
    count = lax.axis_size("col")
    if block % 128 or count % 2 or count < 4:
        share = lax.psum_scatter(partial_value, "col", scatter_dimension=0, tiled=True)
    else:
        share = ring_sum(partial_value, count)
    shares = lax.all_gather(share, ("row", "col"), axis=0, tiled=True)
    parts = rows
    if block % 128:
        shares = assembled(shares.reshape(rows, -1, block), rows, block)
        parts = 1

    width = panel.shape[1] // rows
    slab = lax.dynamic_slice_in_dim(panel, me * width, width, axis=1)
    update = chain(shares, slab, factor, parts)
    update = lax.all_to_all(update, "row", 0, 1, tiled=True)
    return (update, buffer)


def solution(mesh):
    def whole(gradient, momentum):
        factor = 0.2 * math.sqrt(max(gradient.shape))
        return jax.shard_map(
            functools.partial(per_device, factor),
            mesh=mesh,
            in_specs=(P("row", "col"), P("row", "col")),
            out_specs=(P("row", "col"), P("row", "col")),
            check_vma=False,
        )(gradient, momentum)

    return whole
```
